256 devices in a mesh: gx: 32 (over x, y, core), gy: 8 (over z).
Axes of the slice: x: 4, y: 4, z: 8, core: 2. Of those that a mesh axis runs over, the one named last changes fastest.
Arguments:
- atmosphere_state: bfloat16 [128, 800, 1600], P('gy', 'gx'), may hold values from -6 to 6
- forcing: float32 [128], P('gy'), may hold values from -4 to 4
- mixing: float32 [4, 32, 32], replicated, may hold values from -1 to 1
- order_slot: int32 [800], replicated, may hold values from 0 to 799, each once
- legendre: bfloat16 [800, 800, 800], P('gx', None, 'gy'), may hold values from -0.21875 to 0.21875
- ocean_tracer: float32 [8, 512, 8192], P(None, 'gy', 'gx'), may hold values from -6 to 6
- kinetic: float32 [8, 512, 8192], P(None, 'gy', 'gx'), may hold values from 0.01 to 1
- dissipation: float32 [8, 512, 8192], P(None, 'gy', 'gx'), may hold values from 0.001 to 0.1
- wet_mask: int32 [512, 8192], P('gy', 'gx'), may hold values 0 or 1
- send_cell: int32 [8, 163840], P('gy', 'gx'), may hold values from 0 to 16383
- send_weight: float32 [8, 163840], P('gy', 'gx'), may hold values from 0.5 to 2
- receive_cell: int32 [8, 163840], P('gy', 'gx'), may hold values from 0 to 39999
- wind_source: int32 [8, 163840], P('gy', 'gx'), may hold values from 0 to 39999
- wind_target: int32 [8, 163840], P('gy', 'gx'), may hold values from 0 to 16383
- wind_count: int32 [8, 32, 32], P('gy', 'gx'), may hold values from 1 to 160, 2560 in all within a row
Outputs:
- spectral: float32 [800, 800, 256], P('gx', 'gy')
- tracer_out: float32 [8, 512, 8192], P(None, 'gy', 'gx')
The draws below stay inside these ranges and needn't reach their ends.
Inputs may be any that keep to these rules, and one draw needn't show every extreme that they name: `wind_count`: for every tile some band sends exactly 160 live slots.
All inputs are finite; a program needn't handle non-finite values. No bound on the sum of `wet_mask` on one device may be relied on, other than what follows from the above.
Results may differ from the reference program's by a relative error of at most 0.0035.
The reference program's roundings to bfloat16 on the way (of `forced`, `wind`, `table` and `fourier`) count: a program that leaves them out, or rounds other values in their place, can miss the bound.
Values may be sent and summed in bfloat16 or wider, within the bound.
No kernel may reach another device: no remote copies, remote signals or barrier semaphores. Data moves between devices by JAX's collectives and lax.ppermute only.
A program may use at most 128 MiB of HBM per device.

```python
import math
import jax
import jax.numpy as jnp
import numpy as np
from jax import lax

NLAT = 800
NLON = 1600
ORDERS = 800
NDEG = 800
NVAR = 4
LEV = 32
OLAY = 8
OSTEPS = 4
OCEAN_TILE_ROWS = 64
OCOL_DEV = 256
CAP = 160
RCAP = 160
FIELDS = 128
LAT_DEV = 25
ORD_DEV = 25
OROWS = 512
OCOLS = 8192
N_GX = 32
N_GY = 8


def touch_ends(drawn, own_key, smallest, largest):
    spot = [jax.random.randint(jax.random.fold_in(own_key, axis), (), 0, length) for axis, length in enumerate(drawn.shape)]
    widest = drawn.shape.index(max(drawn.shape))
    neighbour = spot[:widest] + [(spot[widest] + 1) % drawn.shape[widest]] + spot[widest + 1:]
    return drawn.at[tuple(spot)].set(smallest).at[tuple(neighbour)].set(largest)


def shard_levels(stream_key, shape, pieces, smallest, largest):
    gain = 1.0
    for axis_at, shards_of in pieces:
        draws = jax.random.uniform(jax.random.fold_in(jax.random.fold_in(stream_key, 6), axis_at), (shards_of,), jnp.float32, smallest / len(pieces), largest / len(pieces))
        gain = gain * jnp.repeat(jnp.exp(draws), shape[axis_at] // shards_of).reshape((-1,) + (1,) * (len(shape) - 1 - axis_at))
    return gain


def length_profile(amount, total, reach, slope):
    weights = [(1 << 20) // math.isqrt(standing ** slope) + 1 for standing in range(2, amount + 1)]
    rest, given = total - reach - (amount - 1), [1] * (amount - 1)
    while rest > 0:
        free = [i for i in range(amount - 1) if given[i] < reach]
        mass, left = sum([weights[i] for i in free]), rest
        for i in free:
            extra = min(reach - given[i], max(1, left * weights[i] // mass), rest)
            given[i] = given[i] + extra
            rest = rest - extra
    return np.array([reach] + given)


def ragged(stream_key, number_of, total, limit, slope):
    if number_of == 2:
        one = jax.random.randint(stream_key, (), max(1, total - limit), min(limit, total - 1) + 1)
        return jnp.stack([one, total - one])
    lengths = jnp.asarray(length_profile(number_of, total, limit, slope), jnp.int32)
    couples = (number_of - 1) // 2
    source_of, receiver = lengths[1:1 + 2 * couples:2], lengths[2:2 + 2 * couples:2]
    slack = jnp.minimum(source_of - 1, limit - receiver)
    passed = jax.random.randint(jax.random.fold_in(stream_key, 1), (couples,), 0, 1 << 20) % (slack + 1)
    lengths = lengths.at[1:1 + 2 * couples:2].set(source_of - passed).at[2:2 + 2 * couples:2].set(receiver + passed)
    return lengths[jax.random.permutation(jax.random.fold_in(stream_key, 2), number_of)]


def bell_draw(stream_key, extent, width, bound, shards=(), kind=jnp.bfloat16):
    entries = width * jax.random.normal(stream_key, extent, jnp.float32)
    if shards:
        entries = entries * shard_levels(stream_key, extent, shards, -0.22, 0.18)
    return jnp.clip(entries, -bound, bound).astype(kind)


def setup_inputs(seed: int = 0) -> dict:
    keys = jax.random.split(jax.random.key(seed), 16)
    return {
        "atmosphere_state": bell_draw(keys[0], (FIELDS, NLAT, NLON), 1.0, 6.0, ((0, 8), (1, 32))),
        "forcing": bell_draw(keys[1], (FIELDS,), 1.0, 4.0, ((0, 8),), jnp.float32),
        "mixing": bell_draw(keys[2], (NVAR, LEV, LEV), LEV ** -0.5, 1.0, (), jnp.float32),
        "order_slot": jax.random.permutation(keys[3], ORDERS).astype(jnp.int32),
        "legendre": bell_draw(keys[4], (ORDERS, NLAT, NDEG), NLAT ** -0.5, 0.21875, ((0, 32), (2, 8))),
        "ocean_tracer": bell_draw(keys[5], (OLAY, OROWS, OCOLS), 1.0, 6.0, ((1, 8), (2, 32)), jnp.float32),
        "kinetic": jnp.clip(jnp.exp(math.log(1.0) - 4.6051702 * jax.random.uniform(keys[6], (OLAY, OROWS, OCOLS), jnp.float32) ** shard_levels(keys[6], (OLAY, OROWS, OCOLS), ((1, 8), (2, 32)), -0.2, 0.2)), 0.01, 1.0),
        "dissipation": jnp.clip(jnp.exp(math.log(0.1) - 4.6051702 * jax.random.uniform(keys[7], (OLAY, OROWS, OCOLS), jnp.float32) ** shard_levels(keys[7], (OLAY, OROWS, OCOLS), ((1, 8), (2, 32)), -0.2, 0.2)), 0.001, 0.1),
        "wet_mask": touch_ends((jax.random.randint(keys[8], (OROWS, OCOLS), 0, 10) < 7).astype(jnp.int32), jax.random.fold_in(keys[8], 1), 0, 1),
        "send_cell": touch_ends(jax.random.randint(keys[9], (N_GY, N_GX * N_GX * CAP), 0, OCEAN_TILE_ROWS * OCOL_DEV), jax.random.fold_in(keys[9], 1), 0, (OCEAN_TILE_ROWS * OCOL_DEV) - 1).astype(jnp.int32),
        "send_weight": jnp.clip(jnp.exp(math.log(2.0) - 1.3862944 * jax.random.uniform(keys[10], (N_GY, N_GX * N_GX * CAP), jnp.float32) ** shard_levels(keys[10], (N_GY, N_GX * N_GX * CAP), ((0, 8), (1, 32)), -0.2, 0.2)), 0.5, 2.0),
        "receive_cell": touch_ends(jax.random.randint(keys[11], (N_GY, N_GX * N_GX * CAP), 0, LAT_DEV * NLON), jax.random.fold_in(keys[11], 1), 0, (LAT_DEV * NLON) - 1).astype(jnp.int32),
        "wind_source": touch_ends(jax.random.randint(keys[12], (N_GY, N_GX * N_GX * RCAP), 0, LAT_DEV * NLON), jax.random.fold_in(keys[12], 1), 0, (LAT_DEV * NLON) - 1).astype(jnp.int32),
        "wind_target": touch_ends(jax.random.randint(keys[13], (N_GY, N_GX * N_GX * RCAP), 0, OCEAN_TILE_ROWS * OCOL_DEV), jax.random.fold_in(keys[13], 1), 0, (OCEAN_TILE_ROWS * OCOL_DEV) - 1).astype(jnp.int32),
        "wind_count": jax.vmap(lambda own: ragged(own, N_GX, N_GX * RCAP // 2, RCAP, 2))(jax.random.split(keys[14], N_GY * N_GX)).reshape((N_GY, N_GX, N_GX)).astype(jnp.int32),
    }


mix_coeff = 0.12
wind_coeff = 0.5

def order_table(order_slot, longitudes):
    lon_index = jnp.arange(longitudes, dtype=jnp.int32)
    phase = lon_index[:, None] * order_slot[None, :].astype(jnp.int32) % longitudes
    angle = phase.astype(jnp.float32) * (2.0 * math.pi / longitudes)
    scale = 1.0 / math.sqrt(longitudes)
    return jnp.stack([jnp.cos(angle) * scale, -jnp.sin(angle) * scale], axis=1).astype(jnp.bfloat16)

def relax(tracer, wetf, vface, padded):
    layers = tracer.shape[0]
    rows = tracer.shape[1]
    cols = tracer.shape[2]
    change = jnp.zeros_like(tracer)
    for row_shift, col_shift in ((0, 1), (2, 1), (1, 0), (1, 2)):
        nearby = padded[:, row_shift:row_shift + rows, col_shift:col_shift + cols]
        change = change + mix_coeff * wetf * nearby[layers] * (nearby[:layers] - tracer)
    flux = vface * (tracer[1:] - tracer[:-1])
    change = change.at[:-1].add(flux).at[1:].add(-flux)
    return tracer + change

def reference(atmosphere_state, forcing, mixing, order_slot, legendre, ocean_tracer, kinetic, dissipation, wet_mask, send_cell, send_weight, receive_cell, wind_source, wind_target, wind_count):
    band_cells = LAT_DEV * NLON
    tile_cells = OCEAN_TILE_ROWS * OCOL_DEV
    wetf = wet_mask.astype(jnp.float32)

    def scatter_to_tiles(field):
        return field.reshape(N_GY, OCEAN_TILE_ROWS, N_GX, OCOL_DEV).transpose(0, 2, 1, 3).reshape(N_GY, N_GX, tile_cells)

    def from_tiles(field):
        return field.reshape(N_GY, N_GX, OCEAN_TILE_ROWS, OCOL_DEV).transpose(0, 2, 1, 3).reshape(OROWS, OCOLS)
    sea = scatter_to_tiles(ocean_tracer[0] * wetf)
    row_pick = jnp.arange(N_GY, dtype=jnp.int32)[:, None, None, None]
    col_pick = jnp.arange(N_GX, dtype=jnp.int32)[None, :, None, None]
    offers = sea[row_pick, col_pick, send_cell.reshape(N_GY, N_GX, N_GX, CAP)] * send_weight.reshape(N_GY, N_GX, N_GX, CAP)
    arrived = offers.transpose(0, 2, 1, 3)
    band_pick = jnp.arange(N_GX, dtype=jnp.int32)[None, :, None, None]
    target_cells = band_pick * band_cells + receive_cell.reshape(N_GY, N_GX, N_GX, CAP)
    surface_fields = jnp.zeros((NLAT * NLON,), jnp.float32).at[target_cells.reshape(-1)].add(arrived.reshape(-1)).reshape(NLAT, NLON)
    forced = (atmosphere_state.astype(jnp.float32) + forcing[:, None, None] * surface_fields[None]).astype(jnp.bfloat16)
    lower = forced[:2 * LEV].astype(jnp.float32).reshape(2, LEV, NLAT * NLON)
    wind = jnp.einsum('wl,wlc->wc', mixing[:2, 0, :], lower, precision=lax.Precision.HIGHEST).astype(jnp.bfloat16)
    table = order_table(order_slot, NLON).reshape(NLON, 2 * ORDERS)
    fourier = jnp.einsum('fal,lc->fca', forced.astype(jnp.float32), table.astype(jnp.float32)).astype(jnp.bfloat16)
    four_blocks = fourier.reshape(FIELDS, 2, N_GX, ORD_DEV, NLAT).transpose(2, 0, 1, 3, 4)
    legendre_blocks = legendre.reshape(N_GX, ORD_DEV, NLAT, NDEG)
    order_blocks = order_slot.reshape(N_GX, ORD_DEV)
    degree = jnp.arange(NDEG, dtype=jnp.int32)

    def one_block(inputs):
        four_part, table_part, order_part = inputs
        masked = jnp.where(degree[None, None, :] >= order_part[:, None, None], table_part, jnp.zeros_like(table_part))
        unmixed_values = jnp.einsum('frsl,sln->snfr', four_part.astype(jnp.float32), masked.astype(jnp.float32))
        unmixed_values = unmixed_values.reshape(ORD_DEV, NDEG, NVAR, LEV, 2)
        mixed_tracer = jnp.einsum('hkz,fchzu->fchku', mixing, unmixed_values, precision=lax.Precision.HIGHEST)
        return mixed_tracer.reshape(ORD_DEV, NDEG, FIELDS * 2)
    spectral = lax.map(one_block, (four_blocks, legendre_blocks, order_blocks)).reshape(ORDERS, NDEG, FIELDS * 2)
    source_band = jnp.arange(N_GX, dtype=jnp.int32)[None, None, :, None]
    global_cell = source_band * band_cells + wind_source.reshape(N_GY, N_GX, N_GX, RCAP)
    fetched = wind[:, global_cell].astype(jnp.float32)
    live = (jnp.arange(RCAP, dtype=jnp.int32)[None, None, None, :] < wind_count[:, :, :, None]).astype(jnp.float32)
    tile_pick = (jnp.arange(N_GY, dtype=jnp.int32)[:, None, None, None] * N_GX + jnp.arange(N_GX, dtype=jnp.int32)[None, :, None, None]) * tile_cells
    placed = tile_pick + wind_target.reshape(N_GY, N_GX, N_GX, RCAP)
    ocean_wind = jnp.zeros((2, N_GY * N_GX * tile_cells), jnp.float32).at[:, placed.reshape(-1)].add((fetched * live[None]).reshape(2, -1))
    east_wind = from_tiles(ocean_wind[0])
    north_wind = from_tiles(ocean_wind[1])
    speed = east_wind ** 2 + north_wind ** 2
    energy = kinetic.at[0].add(wind_coeff * speed)
    ratio = 0.09 * energy * energy / dissipation
    viscosity = 0.25 * ratio / (1.0 + ratio)
    vface = 0.5 * (viscosity[:-1] + viscosity[1:]) * wetf[None]
    tracer = ocean_tracer
    for sub_step in range(OSTEPS):
        stacked = jnp.concatenate([tracer, wetf[None]], axis=0)
        padded = jnp.pad(stacked, ((0, 0), (1, 1), (1, 1)))
        tracer = relax(tracer, wetf, vface, padded)
    return (spectral, tracer)
```

```python
import functools
import math

import jax
import jax.numpy as jnp
from jax import lax
from jax.experimental import pallas as pl
from jax.experimental.pallas import tpu as pltpu
from jax.sharding import PartitionSpec as P

OSTEPS = 4
mix_coeff = 0.12
wind_coeff = 0.5

BF = jnp.bfloat16
F32 = jnp.float32
I32 = jnp.int32
NT = (((1,), (1,)), ((), ()))
NN = (((1,), (0,)), ((), ()))

CHUNKS = ((0, 13), (13, 12))
SP = 16
LONS = 1600
LON_PAD = 1664
TILES = 13
BAND = 32
QLANES = 1664
ROWS = 512


def split2(x):
    hi = x.astype(BF)
    return hi, (x - hi.astype(F32)).astype(BF)


def iota(shape, dim):
    return lax.broadcasted_iota(I32, shape, dim)


def row_call(body, outs, scratch=(), **kw):
    return pl.pallas_call(body, out_shape=outs, scratch_shapes=list(scratch), **kw)


def turn_cos(turns):
    near = turns - jnp.floor(turns + 0.5)
    w = 0.25 - jnp.abs(near)
    u = w * w
    acc = jnp.full_like(u, -((2 * math.pi) ** 11) / math.factorial(11))
    for power in (9, 7, 5, 3, 1):
        sign = 1.0 if power % 4 == 1 else -1.0
        acc = acc * u + sign * (2 * math.pi) ** power / math.factorial(power)
    return acc * w


def table_rows(order, quarter, out_ref):
    lanes = iota(order.shape, 1)
    raw = (order * lanes).astype(F32) + quarter
    turns = raw * (1.0 / LONS)
    turns = turns - jnp.floor(turns)
    step = (order * 128).astype(F32) * (1.0 / LONS)
    step = step - jnp.floor(step)
    scale = 1.0 / math.sqrt(LONS)
    c = turn_cos(turns) * scale
    s = turn_cos(turns - 0.25) * scale
    dc = turn_cos(step)
    ds = turn_cos(step - 0.25)
    for t in range(TILES):
        out_ref[:, t * 128 : (t + 1) * 128] = c.astype(BF)
        if t + 1 < TILES:
            c, s = c * dc - s * ds, s * dc + c * ds


def fourier_body(with_base, order_ref, state_ref, *refs):
    if with_base:
        pick_ref, four_ref, table_ref, base_ref, laid = refs
    else:
        four_ref, table_ref, laid = refs

    @pl.when(pl.program_id(0) == 0)
    def _():
        flat = state_ref[...].reshape(400, LONS)
        r = iota((512, 400), 0)
        c = iota((512, 400), 1)
        move = ((r // 32 == c % 16) & (r % 32 == c // 16)).astype(F32).astype(BF)
        laid[:, 1536:] = jnp.zeros((512, 128), BF)
        laid[:, :LONS] = lax.dot_general(move, flat, NN, preferred_element_type=F32).astype(BF)
        if with_base:
            r = iota((64, 400), 0)
            c = iota((64, 400), 1)
            here = r % 32 == c // 16
            w = jnp.where(here, pick_ref[...], 0.0)
            hi, lo = split2(w)
            base_ref[...] = jnp.zeros((64, LON_PAD), F32)
            base_ref[:, :LONS] = lax.dot_general(
                hi, flat, NN, preferred_element_type=F32
            ) + lax.dot_general(lo, flat, NN, preferred_element_type=F32)

    order = jnp.broadcast_to(order_ref[...], (128, 128))
    quarter = ((iota((128, 128), 0) // SP) % 2).astype(F32) * 400.0
    table_rows(order, quarter, table_ref)
    four_ref[...] = lax.dot_general(
        table_ref[...], laid[...], NT, preferred_element_type=F32
    ).astype(BF)


def fourier_chunk(order_rows, state, pick):
    rows = order_rows.shape[0]
    with_base = pick is not None
    in_specs = [
        pl.BlockSpec((128, 1), lambda g: (g, 0)),
        pl.BlockSpec((25, 16, LONS), lambda g: (0, 0, 0)),
    ]
    out_specs = [
        pl.BlockSpec((128, 512), lambda g: (g, 0)),
        pl.BlockSpec((128, LON_PAD), lambda g: (g, 0)),
    ]
    outs = [
        jax.ShapeDtypeStruct((rows, 512), BF),
        jax.ShapeDtypeStruct((rows, LON_PAD), BF),
    ]
    args = [order_rows, state]
    if with_base:
        in_specs.append(pl.BlockSpec((64, 400), lambda g: (0, 0)))
        out_specs.append(pl.BlockSpec((64, LON_PAD), lambda g: (0, 0)))
        outs.append(jax.ShapeDtypeStruct((64, LON_PAD), F32))
        args.append(pick)
    return pl.pallas_call(
        functools.partial(fourier_body, with_base),
        grid=(rows // 128,),
        in_specs=in_specs,
        out_specs=out_specs,
        out_shape=outs,
        scratch_shapes=[pltpu.VMEM((512, LON_PAD), BF)],
        name="fourier_base" if with_base else "fourier",
    )(*args)


def lay_body(ns, in_ref, out_ref, rows, rest):
    lanes = iota((SP, 128), 1)

    def one(step, _):
        r = step // 4
        high = step % 4
        tile = in_ref[:, pl.ds(pl.multiple_of(r * SP, SP), SP), pl.ds(pl.multiple_of(high * 128, 128), 128)]
        tile = tile.astype(F32)
        for low in range(4):
            acc = [jnp.zeros((SP, 128), F32) for _ in range(7)]
            for band in range(32):
                start = 25 * band
                at, off = start // 128, start % 128
                shift = (off - 32 * low) % 128
                piece = pltpu.roll(tile[band], shift, 1) if shift else tile[band]
                acc[at] = jnp.where((lanes >= off) & (lanes < off + 25), piece, acc[at])
                if off + 25 > 128:
                    acc[at + 1] = jnp.where(lanes < off + 25 - 128, piece, acc[at + 1])
            f = high * 4 + low
            for t in range(6):
                rows[pl.ds(r * 6 + t, 1), pl.ds(f, SP, stride=16), :] = acc[t][None]
            rest[pl.ds(r, 1), pl.ds(f, SP, stride=16), :] = acc[6][None]
        return 0

    lax.fori_loop(0, 8, one, 0)
    for s in range(ns):
        span = pl.ds(s * 16, 16)
        for t in range(6):
            out_ref[s, :, t * 128 : (t + 1) * 128] = rows[t, span, :].astype(BF)
            out_ref[s, :, (t + 7) * 128 : (t + 8) * 128] = rows[t + 6, span, :].astype(BF)
        last = rest[0, span, :] + pltpu.roll(rest[1, span, :], 32, 1)
        out_ref[s, :, 6 * 128 : 7 * 128] = last.astype(BF)


def lay_out(moved, ns):
    return row_call(
        functools.partial(lay_body, ns),
        jax.ShapeDtypeStruct((ns, 16, QLANES), BF),
        (pltpu.VMEM((12, SP * 16, 128), F32), pltpu.VMEM((2, SP * 16, 128), F32)),
        name="lay_out",
    )(moved)


def legendre_body(chunk, first, where_ref, order_ref, *refs):
    pieces = refs[:8]
    leg_ref, moved_ref, mix_ref, coef_ref, out_ref, surf, surf_f, wide = refs[8:]
    step = pl.program_id(0)

    @pl.when(step == 0)
    def _():
        surf_f[800:896, :] = jnp.zeros((96, 128), F32)
        for band in range(32):
            surf_f[25 * band : 25 * band + 25, :] = moved_ref[band, 0:32, :].astype(F32)[0:25]
        surf[...] = surf_f[...].astype(BF)
        wide[...] = jnp.zeros((100, 896), BF)

    order = order_ref[first + step]
    degree = where_ref[0] * 100 + iota((100, 800), 0)
    leg = leg_ref[0].astype(F32)
    wide[:, 0:800] = jnp.where(degree >= order, leg, 0.0).astype(BF)
    leg0 = wide[...]
    tail = pltpu.roll(leg0[:, 768:896].astype(F32), 32, 1).astype(BF)
    leg1 = jnp.concatenate([tail, leg0[:, 0:768]], axis=1)
    x = jnp.concatenate([p[0] for p in pieces], axis=0)
    raw0 = lax.dot_general(leg0, x[:, 0:896], NT, preferred_element_type=F32)
    raw1 = lax.dot_general(leg1, x[:, 768:1664], NT, preferred_element_type=F32)
    seen = lax.dot_general(leg0, surf[...], NN, preferred_element_type=F32)
    raw = jnp.concatenate([raw0, raw1], axis=1)
    hi, lo = split2(raw)
    out = lax.dot_general(
        jnp.concatenate([hi, lo, hi], axis=1), mix_ref[...], NN, preferred_element_type=F32
    )
    lane = iota((100, 128), 1) % 64
    for r in range(2):
        column = chunk * 32 + r * SP + step
        part = jnp.sum(jnp.where(lane == column, seen, 0.0), axis=1, keepdims=True)
        out = out + part * coef_ref[r : r + 1, :]
    out_ref[0] = out


def legendre_chunk(chunk, pieces, leg, moved, mix, coef, my_orders, plane):
    first, ns = CHUNKS[chunk]
    grid = pltpu.PrefetchScalarGridSpec(
        num_scalar_prefetch=2,
        grid=(ns,),
        in_specs=[pl.BlockSpec((1, 16, QLANES), lambda s, *_: (s, 0, 0))] * 8
        + [
            pl.BlockSpec((1, 100, 800), lambda s, *_: (s + first, 0, 0)),
            pl.BlockSpec((32, 48, 128), lambda s, *_: (0, 0, 0)),
            pl.BlockSpec((768, 256), lambda s, *_: (0, 0)),
            pl.BlockSpec((8, 256), lambda s, *_: (0, 0)),
        ],
        out_specs=pl.BlockSpec((1, 100, 256), lambda s, *_: (s, 0, 0)),
        scratch_shapes=[
            pltpu.VMEM((896, 128), BF),
            pltpu.VMEM((896, 128), F32),
            pltpu.VMEM((100, 896), BF),
        ],
    )
    return pl.pallas_call(
        functools.partial(legendre_body, chunk, first),
        grid_spec=grid,
        out_shape=jax.ShapeDtypeStruct((ns, 100, 256), F32),
        name="legendre",
    )(plane, my_orders, *pieces, leg, moved, mix, coef)


def offers_body(tracer_ref, wet_ref, cell_ref, weight_ref, ask_ref, out_ref):
    sea = tracer_ref[0] * wet_ref[...].astype(F32)
    hi, lo = split2(sea)
    sea2 = jnp.concatenate([hi, lo], axis=0)

    def one(k, _):
        cell = cell_ref[pl.ds(k, 1), :]
        low = jnp.broadcast_to(cell & 255, (256, 256))
        hot = (low == iota((256, 256), 0)).astype(F32).astype(BF)
        got = lax.dot_general(sea2, hot, NN, preferred_element_type=F32)
        got = got[0:64] + got[64:128]
        high = jnp.broadcast_to(cell >> 8, (64, 256))
        value = jnp.sum(jnp.where(high == iota((64, 256), 0), got, 0.0), axis=0, keepdims=True)
        value = value * weight_ref[pl.ds(k, 1), :]
        ask = ask_ref[pl.ds(k, 1), :].astype(F32)
        rows = [value[:, :128], value[:, 128:], ask[:, :128], ask[:, 128:]]
        tile = jnp.zeros((8, 128), F32)
        for i, row in enumerate(rows):
            tile = jnp.where(iota((8, 128), 0) == i, row, tile)
        out_ref[pl.ds(k, 1)] = tile[None]
        return 0

    lax.fori_loop(0, 32, one, 0, unroll=4)


def offers(tracer, wet, cells, weights, asks):
    whole = lambda shape: pl.BlockSpec(shape, lambda g: (0,) * len(shape))
    return pl.pallas_call(
        offers_body,
        grid=(1,),
        in_specs=[whole((1, 64, 256)), whole((64, 256))] + [whole((32, 256))] * 3,
        out_specs=whole((32, 8, 128)),
        out_shape=jax.ShapeDtypeStruct((32, 8, 128), F32),
        name="offers",
    )(tracer, wet, cells, weights, asks)


def surface_body(got_ref, high_ref, low_ref, base_ref, extra_ref, out_ref, acc):
    acc[...] = jnp.zeros((416, 256), F32)

    def one(g, _):
        k = g * 4
        value = jnp.concatenate(
            [got_ref[k + i, j : j + 1, :] for i in range(4) for j in range(2)], axis=1
        )
        high = jnp.concatenate([high_ref[pl.ds(k + i, 1), :] for i in range(4)], axis=1)
        low = jnp.concatenate([low_ref[pl.ds(k + i, 1), :] for i in range(4)], axis=1)
        hot = (jnp.broadcast_to(high, (416, 1024)) == iota((416, 1024), 0)).astype(F32).astype(BF)
        here = jnp.broadcast_to(low, (128, 1024)) == iota((128, 1024), 0)
        v = jnp.where(here, jnp.broadcast_to(value, (128, 1024)), 0.0)
        hi, lo = split2(v)
        acc[...] += lax.dot_general(
            hot, jnp.concatenate([hi, lo], axis=0), NT, preferred_element_type=F32
        )
        return 0

    lax.fori_loop(0, 8, one, 0)
    for t in range(16):
        at = (t // 2, slice((t % 2) * 32, (t % 2) * 32 + 32))
        if t < TILES:
            s = acc[t * 32 : t * 32 + 32, 0:128] + acc[t * 32 : t * 32 + 32, 128:256]
            winds = [base_ref[w * 32 : w * 32 + 32, t * 128 : t * 128 + 128] for w in range(2)]
        else:
            s = extra_ref[...] if t == TILES else jnp.zeros((32, 128), F32)
            winds = [jnp.zeros((32, 128), F32)] * 2
        hi, lo = split2(s)
        out_ref[at[0], 0, at[1], :] = hi
        out_ref[at[0], 1, at[1], :] = lo
        for w in range(2):
            out_ref[at[0], 2 + w, at[1], :] = winds[w].astype(BF)


def surface_parts(got, high, low, base, extra):
    return row_call(
        surface_body,
        jax.ShapeDtypeStruct((8, 4, 64, 128), BF),
        (pltpu.VMEM((416, 256), F32),),
        name="surface_parts",
    )(got, high, low, base, extra)


def total_body(in_ref, out_ref):
    planes = []
    for p in range(4):
        total = in_ref[0, p].astype(F32)
        for j in range(1, 8):
            total = total + in_ref[j, p].astype(F32)
        planes.append(total)
    hi, lo = split2(planes[0] + planes[1])
    for j in range(8):
        out_ref[j, 0] = hi
        out_ref[j, 1] = lo
        out_ref[j, 2] = planes[2].astype(BF)
        out_ref[j, 3] = planes[3].astype(BF)


def total(parts):
    return row_call(total_body, jax.ShapeDtypeStruct((8, 4, 64, 128), BF), name="total")(parts)


def answer_body(all_ref, ask_ref, ta_ref, tb_ref, out_ref, lhs, winds):
    @pl.when(pl.program_id(0) == 0)
    def _():
        gains = []
        for w in range(2):
            row = w
            gains.append(
                all_ref[6, 0, 32 : 48, :].astype(F32)[row : row + 1]
                + all_ref[6, 1, 32 : 48, :].astype(F32)[row : row + 1]
            )
        for t in range(TILES):
            span = slice((t % 2) * 32, (t % 2) * 32 + 32)
            hi = all_ref[t // 2, 0, span, :]
            lo = all_ref[t // 2, 1, span, :]
            lhs[0:32, t * 128 : t * 128 + 128] = hi
            lhs[32:64, t * 128 : t * 128 + 128] = lo
            s = hi.astype(F32) + lo.astype(F32)
            for w in range(2):
                wind = all_ref[t // 2, 2 + w, span, :].astype(F32) + gains[w] * s
                winds[w * 416 + t * 32 : w * 416 + t * 32 + 32, :] = wind.astype(BF)

    both = []
    for ref in (ta_ref, tb_ref):
        f = lax.dot_general(lhs[...], ref[...], NT, preferred_element_type=F32)
        both.append(f[0:32] + f[32:64])
    lanes = iota((32, 128), 1)
    row = iota((16, 128), 0)
    for k in range(4):
        ask = ask_ref[k, 2:4, :]
        ask = jnp.concatenate([ask[0:1], ask[1:2]], axis=1)
        cell = jnp.maximum(ask, 0.0).astype(I32)
        low = jnp.broadcast_to(cell & 127, (128, 256))
        hot = (low == iota((128, 256), 0)).astype(F32).astype(BF)
        got = lax.dot_general(winds[...], hot, NN, preferred_element_type=F32)
        high = jnp.broadcast_to(cell >> 7, (416, 256)) == iota((416, 256), 0)
        tile = jnp.zeros((16, 128), F32)
        for w in range(2):
            value = jnp.sum(
                jnp.where(high, got[w * 416 : w * 416 + 416], 0.0), axis=0, keepdims=True
            )
            tile = jnp.where(row == 2 * w, value[:, :128], tile)
            tile = jnp.where(row == 2 * w + 1, value[:, 128:], tile)
        a = pltpu.roll(both[0], (-32 * k) % 128, 1) if k else both[0]
        b = pltpu.roll(both[1], (32 - 32 * k) % 128, 1) if k != 1 else both[1]
        v = jnp.where(lanes < 32, a, b)
        hi = v.astype(BF).astype(F32)
        out_ref[k, 0:32, :] = jnp.where(lanes < 64, hi, pltpu.roll(v - hi, 64, 1)).astype(BF)
        out_ref[k, 32:48, :] = tile.astype(BF)


def answers(everything, asked, ta, tb):
    return pl.pallas_call(
        answer_body,
        grid=(8,),
        in_specs=[
            pl.BlockSpec((8, 4, 64, 128), lambda g: (0, 0, 0, 0)),
            pl.BlockSpec((4, 8, 128), lambda g: (g, 0, 0)),
            pl.BlockSpec((128, LON_PAD), lambda g: (g, 0)),
            pl.BlockSpec((128, LON_PAD), lambda g: (g, 0)),
        ],
        out_specs=pl.BlockSpec((4, 48, 128), lambda g: (g, 0, 0)),
        out_shape=jax.ShapeDtypeStruct((32, 48, 128), BF),
        scratch_shapes=[pltpu.VMEM((64, LON_PAD), BF), pltpu.VMEM((832, 128), BF)],
        name="answers",
    )(everything, asked, ta, tb)


def face_body(moved_ref, target_ref, kin_ref, dis_ref, wet_ref, out_ref, acc):
    acc[...] = jnp.zeros((128, 256), F32)

    def one(g, _):
        k = g * 4
        tiles = [moved_ref[k + i, 32:48, :].astype(F32) for i in range(4)]
        spot = jnp.concatenate([target_ref[pl.ds(k + i, 1), :] for i in range(4)], axis=1)
        col = jnp.broadcast_to(spot & 255, (256, 1024)) == iota((256, 1024), 0)
        col = col.astype(F32).astype(BF)
        row = jnp.broadcast_to(spot >> 8, (64, 1024)) == iota((64, 1024), 0)
        parts = []
        for w in range(2):
            value = jnp.concatenate(
                [t[2 * w + j : 2 * w + j + 1] for t in tiles for j in range(2)], axis=1
            )
            parts.append(jnp.where(row, jnp.broadcast_to(value, (64, 1024)), 0.0).astype(BF))
        acc[...] += lax.dot_general(
            jnp.concatenate(parts, axis=0), col, NT, preferred_element_type=F32
        )
        return 0

    lax.fori_loop(0, 8, one, 0)
    east = acc[0:64]
    north = acc[64:128]
    speed = east * east + north * north

    def viscosity(energy, dissipation):
        ratio = 0.09 * energy * energy / dissipation
        return 0.25 * ratio / (1.0 + ratio)

    top = viscosity(kin_ref[0] + wind_coeff * speed, dis_ref[0])
    below = viscosity(kin_ref[1], dis_ref[1])
    out_ref[...] = 0.5 * (top + below) * wet_ref[...].astype(F32)


def top_face(moved, target, kinetic, dissipation, wet):
    whole = lambda shape: pl.BlockSpec(shape, lambda g: (0,) * len(shape))
    return pl.pallas_call(
        face_body,
        grid=(1,),
        in_specs=[
            whole((32, 48, 128)),
            whole((32, 256)),
            whole((2, 64, 256)),
            whole((2, 64, 256)),
            whole((64, 256)),
        ],
        out_specs=whole((64, 256)),
        out_shape=jax.ShapeDtypeStruct((64, 256), F32),
        scratch_shapes=[pltpu.VMEM((128, 256), F32)],
        name="top_face",
    )(moved, target, kinetic, dissipation, wet)


def ocean_body(tracer_ref, face_ref, wet_ref, side_ref, edge_ref, top_ref, top_side, top_edge, out_ref, tr, vf, cw):
    for p in range(15):
        edge = edge_ref[p].astype(F32)
        side = side_ref[p].astype(F32)
        if p < 8:
            tr[p, 0:64, 0:256] = tracer_ref[p]
            tr[p, 0:64, 256:384] = side
            tr[p, 64:72, :] = edge
        elif p < 14:
            vf[p - 7, 0:64, 0:256] = face_ref[p - 8]
            vf[p - 7, 0:64, 256:384] = side
            vf[p - 7, 64:72, :] = edge
        else:
            cw[0, 0:64, 0:256] = wet_ref[...].astype(F32)
            cw[0, 0:64, 256:384] = side
            cw[0, 64:72, :] = edge
    vf[0, 0:64, 0:256] = top_ref[...]
    vf[0, 0:64, 256:384] = top_side[...]
    vf[0, 64:72, :] = top_edge[...]

    def around(x):
        return (
            pltpu.roll(x, 1, 0),
            pltpu.roll(x, 71, 0),
            pltpu.roll(x, 1, 1),
            pltpu.roll(x, 383, 1),
        )

    wet = cw[0]
    for d, near in enumerate(around(wet)):
        cw[d] = mix_coeff * wet * near

    def one(step, _):
        flux = None
        layers = 8
        for l in range(layers):
            x = tr[l]
            new = x
            for d, near in enumerate(around(x)):
                new = new + cw[d] * (near - x)
            if flux is not None:
                new = new - flux
            if l + 1 < layers:
                flux = vf[l] * (tr[l + 1] - x)
                new = new + flux
            tr[l] = new
        return 0

    lax.fori_loop(0, OSTEPS, one, 0)
    out_ref[...] = tr[:, 0:64, 0:256]


def ocean(tracer, face, wet, side, edge, top, top_side, top_edge):
    return row_call(
        ocean_body,
        jax.ShapeDtypeStruct((8, 64, 256), F32),
        (
            pltpu.VMEM((8, 72, 384), F32),
            pltpu.VMEM((7, 72, 384), F32),
            pltpu.VMEM((4, 72, 384), F32),
        ),
        name="ocean",
    )(tracer, face, wet, side, edge, top, top_side, top_edge)


def borders(x):
    lead = (slice(None),) * (x.ndim - 2)
    gx, gy = lax.axis_size("gx"), lax.axis_size("gy")
    up_x = [(i, i + 1) for i in range(gx - 1)]
    up_y = [(i, i + 1) for i in range(gy - 1)]
    from_left = lax.ppermute(x[lead + (slice(None), slice(128, 256))], "gx", up_x)
    from_right = lax.ppermute(x[lead + (slice(None), slice(0, 128))], "gx", [(b, a) for a, b in up_x])
    lane = iota(from_left.shape, x.ndim - 1)
    side = jnp.where(lane < 64, from_right, from_left)
    wide = lambda rows: jnp.concatenate(
        [x[lead + (rows, slice(None))], side[lead + (rows, slice(None))]], axis=-1
    )
    from_below = lax.ppermute(wide(slice(56, 64)), "gy", up_y)
    from_above = lax.ppermute(wide(slice(0, 8)), "gy", [(b, a) for a, b in up_y])
    row = iota(from_below.shape, x.ndim - 2)
    return side, jnp.where(row < 4, from_above, from_below)


def ring(first, second):
    peers = lax.axis_size("gy")
    right = [(i, (i + 1) % peers) for i in range(peers)]
    left = [(b, a) for a, b in right]
    pieces = ([first], [second])
    go = [[first, first], [second, second]]
    for step in range(3):
        for c in range(2):
            go[c][0] = lax.ppermute(go[c][0], "gy", right)
            go[c][1] = lax.ppermute(go[c][1], "gy", left)
            pieces[c].extend(go[c])
    pieces[0].append(lax.ppermute(go[0][0], "gy", right))
    pieces[1].append(lax.ppermute(go[1][1], "gy", left))
    return pieces


def spread(rows, fill):
    return jnp.pad(rows.reshape(32, 160), ((0, 0), (0, 96)), constant_values=fill)


def exchange(x):
    return lax.all_to_all(x, "gx", split_axis=0, concat_axis=0, tiled=True)


def shards(
    atmosphere_state,
    forcing,
    mixing,
    order_slot,
    legendre,
    ocean_tracer,
    kinetic,
    dissipation,
    wet_mask,
    send_cell,
    send_weight,
    receive_cell,
    wind_source,
    wind_target,
    wind_count,
):
    k, j = lax.axis_index("gx"), lax.axis_index("gy")
    wetf = wet_mask.astype(F32)
    state = atmosphere_state.transpose(1, 0, 2)
    leg = legendre.transpose(0, 2, 1)

    select = (jnp.arange(4)[None, :] == jnp.arange(2)[:, None]).astype(F32)
    bottom = (select[:, :, None] * mixing[None, :, 0, :]).reshape(2, 128)
    bottom = lax.dynamic_slice_in_dim(bottom, j * 16, 16, 1)
    pick = jnp.broadcast_to(bottom[:, None, None, :], (2, 32, 25, 16)).reshape(64, 400)
    gain = jnp.sum(bottom * forcing[None, :], axis=1)
    spot = jnp.arange(128) // 16 == j
    extra = jnp.concatenate(
        [
            jnp.broadcast_to(gain[:, None], (2, 128)),
            jnp.where(spot, jnp.tile(forcing, 8), 0.0)[None],
            jnp.zeros((29, 128), F32),
        ],
        axis=0,
    )

    slots = order_slot.reshape(32, 25)

    def chunk_orders(first, ns):
        part = jnp.pad(slots[:, first : first + ns], ((0, 0), (0, SP - ns)))
        return jnp.broadcast_to(part[:, None, :], (32, 2, SP)).reshape(-1, 1)

    four_a, table_a, base = fourier_chunk(chunk_orders(*CHUNKS[0]), state, pick)
    moved_a = exchange(four_a.reshape(32, 2 * SP, 512))
    laid_a = lay_out(moved_a, CHUNKS[0][1])
    four_b, table_b = fourier_chunk(chunk_orders(*CHUNKS[1]), state, None)
    moved_b = exchange(four_b.reshape(32, 2 * SP, 512))
    laid_b = lay_out(moved_b, CHUNKS[1][1])
    pieces_a, pieces_b = ring(laid_a, laid_b)

    asks = spread(wind_source, 0)
    asks = (asks % LONS // 128 * 32 + asks // LONS) * 128 + asks % LONS % 128
    offered = offers(
        ocean_tracer, wet_mask, spread(send_cell, 0), spread(send_weight, 0.0), asks
    )
    got = exchange(offered)
    cell = spread(receive_cell, -1)
    lon = cell % LONS
    high = jnp.where(cell < 0, -1, lon // 128 * 32 + cell // LONS)
    parts = surface_parts(got, high, lon % 128, base, extra)
    sums = total(lax.all_to_all(parts, "gy", split_axis=0, concat_axis=0, tiled=True))
    everything = lax.all_to_all(sums, "gy", split_axis=0, concat_axis=0, tiled=True)
    moved = exchange(answers(everything, got, table_a, table_b))

    force = (everything[6, 0, 34, :].astype(F32) + everything[6, 1, 34, :].astype(F32)).reshape(4, 32)
    coef = jnp.sum(mixing * force[:, None, :], axis=2).reshape(128)
    zero = jnp.zeros_like(coef)
    coef = jnp.stack(
        [jnp.stack([coef, zero], 1).reshape(256), jnp.stack([zero, coef], 1).reshape(256)]
    )
    coef = jnp.pad(coef, ((0, 6), (0, 0)))
    eye = jnp.eye(4, dtype=F32)
    square = (mixing.transpose(0, 2, 1)[:, :, None, :] * eye[:, None, :, None]).reshape(8, 16, 128)
    origin = [0, -1, 1, -2, 2, -3, 3, 4]
    square = jnp.concatenate(
        [lax.dynamic_index_in_dim(square, (j + o) % 8, 0, keepdims=False) for o in origin], axis=0
    )
    none = jnp.zeros_like(square)
    mix = jnp.concatenate(
        [jnp.stack([square, none], 2).reshape(128, 256), jnp.stack([none, square], 2).reshape(128, 256)]
    )
    mix_hi = lax.reduce_precision(mix, 8, 7)
    mix_lo = (mix - mix_hi).astype(BF)
    mix_hi = mix_hi.astype(BF)
    mix = jnp.concatenate([mix_hi, mix_hi, mix_lo], axis=0)
    my_orders = lax.dynamic_slice_in_dim(order_slot, k * 25, 25, 0)
    plane = j.reshape(1).astype(I32)
    spectral = jnp.concatenate(
        [
            legendre_chunk(0, pieces_a, leg, moved, mix, coef, my_orders, plane),
            legendre_chunk(1, pieces_b, leg, moved, mix, coef, my_orders, plane),
        ],
        axis=0,
    )

    ratio = 0.09 * kinetic[1:] * kinetic[1:] / dissipation[1:]
    viscosity = 0.25 * ratio / (1.0 + ratio)
    face = 0.5 * (viscosity[:-1] + viscosity[1:]) * wetf[None]
    side, edge = borders(jnp.concatenate([ocean_tracer, face, wetf[None]], axis=0).astype(BF))
    target = spread(wind_target, 0)
    live = jnp.arange(256, dtype=I32)[None, :] < wind_count.reshape(32, 1)
    target = jnp.where(live, target, -1)
    top = top_face(moved, target, kinetic, dissipation, wet_mask)
    top_side, top_edge = borders(top)
    tracer = ocean(ocean_tracer, face, wet_mask, side, edge, top, top_side, top_edge)
    return (spectral, tracer)


def solution(mesh):
    placed = (
        P("gy", "gx", None),
        P("gy"),
        P(),
        P(),
        P("gx", None, "gy"),
        P(None, "gy", "gx"),
        P(None, "gy", "gx"),
        P(None, "gy", "gx"),
        P("gy", "gx"),
        P("gy", "gx"),
        P("gy", "gx"),
        P("gy", "gx"),
        P("gy", "gx"),
        P("gy", "gx"),
        P("gy", "gx", None),
    )
    return jax.shard_map(
        shards,
        mesh=mesh,
        in_specs=placed,
        out_specs=(P("gx", "gy", None), P(None, "gy", "gx")),
        check_vma=False,
    )
```
